32 devices in a mesh: sep: 4 (over x, core), sub: 8 (over z, y).
Axes of the slice: x: 2, y: 2, z: 4, core: 2. Of those that a mesh axis runs over, the one named last changes fastest.
Arguments:
- g_top: bfloat16 [2048, 2048], P('sub', 'sep'), may hold values from -8 to 32, as said below
- u_mid: bfloat16 [4, 2048, 512], P('sep', 'sub'), may hold values from -0.125 to 0.125
- b_mid: float32 [4, 512, 512], P('sep', 'sub'), may hold values from -8 to 32
- u_leaf: bfloat16 [32, 1536, 1536], P(('sep', 'sub')), may hold values from -0.15625 to 0.15625
- leaf_index: int32 [32, 1536], P(('sep', 'sub')), may hold values from 0 to 2559, as said below
- leaf_count: int32 [32], P(('sep', 'sub')), may hold values from 768 to 1536, as said below
- leaf_bdiag: float32 [32, 1536], P(('sep', 'sub')), may hold values from 4 to 16
Outputs:
- mid_cross: bfloat16 [4, 2048, 512], P('sep', 'sub')
- mid_block: bfloat16 [4, 512, 512], P('sep', 'sub')
- leaf_offdiag: bfloat16 [32, 1536, 1536], P(('sep', 'sub'))
- leaf_diag: float32 [32, 1536], P(('sep', 'sub'))
The draws below stay inside these ranges and needn't reach their ends.
Inputs may be any that keep to these rules, and one draw needn't show every extreme that they name: g_top is symmetric. `leaf_index`: A leaf's 1536 entries are distinct; an entry below 2048 is a row of the top separator, an entry r of 2048 or more is row r - 2048 of the leaf's middle separator. `leaf_count`: some leaf has all 1536 slots live.
All inputs are finite; a program needn't handle non-finite values.
Results may differ from the reference program's by a relative error of at most 0.004.
Values may be sent and summed in bfloat16 or wider, within the bound.
A program may use at most 128 MiB of HBM per device.

```python
import math
import jax
import jax.numpy as jnp
from jax import lax

NT = 2048
NM = 512
BORDER = 1536
LEAF_COLS = 1536
MIDS = 4
LEAVES = 32
N_SUB = 8


def symmetric_draw(member_key, order):
    spread_key, diagonal_key = jax.random.split(member_key)
    spread = jnp.clip(jax.random.normal(spread_key, (order, order), jnp.float32), -3.0, 3.0)
    coupling = (spread + spread.T) * (4.0 / math.sqrt(order))
    diagonal = jax.random.uniform(diagonal_key, (order,), jnp.float32, 8.0, 32.0)
    return jnp.where(jnp.eye(order, dtype=bool), jnp.diag(diagonal), coupling)


def draw_g_top(key, part):
    return symmetric_draw(jax.random.fold_in(key, 11), NT).astype(jnp.bfloat16)


def draw_b_mid(key, part):
    member_keys = jax.random.split(jax.random.fold_in(key, 23), MIDS)
    return jax.vmap(lambda member_key: symmetric_draw(member_key, NM))(member_keys)


def draw_leaf_index(key, part):
    member_keys = jax.random.split(jax.random.fold_in(key, 37), LEAVES)

    def ordering(member_key):
        return jax.random.permutation(member_key, NT + NM)[:BORDER].astype(jnp.int32)
    return jax.vmap(ordering)(member_keys)


def draw_leaf_count(key, part):
    count_key, pick_key = jax.random.split(jax.random.fold_in(key, 41))
    counts = jax.random.randint(count_key, (LEAVES,), BORDER // 2, BORDER + 1, dtype=jnp.int32)
    fullest = jax.random.randint(pick_key, (), 0, LEAVES, dtype=jnp.int32)
    positions = jnp.arange(LEAVES, dtype=jnp.int32)
    return jnp.where(positions == fullest, jnp.int32(BORDER), counts).astype(jnp.int32)


def levels(stream_key, extent, cuts, least, top_value):
    def one(position, shards_of):
        heights = jax.random.uniform(jax.random.fold_in(jax.random.fold_in(stream_key, 6), position), (shards_of,), jnp.float32, least / len(cuts), top_value / len(cuts))
        return jnp.repeat(jnp.exp(heights), extent[position] // shards_of).reshape((-1,) + (1,) * (len(extent) - position - 1))

    loudness = one(*cuts[0])
    for cut in cuts[1:]:
        loudness = loudness * one(*cut)
    return loudness


def gaussian(rng, dims, scale, reach, pieces=(), kind=jnp.bfloat16):
    result = scale * jax.random.normal(rng, dims, jnp.float32)
    if pieces:
        result = result * levels(rng, dims, pieces, -0.22, 0.18)
    return jnp.clip(result, -reach, reach).astype(kind)


def setup_inputs(seed: int = 0) -> dict:
    splits = jax.random.split(jax.random.key(seed), 8)
    g_top = draw_g_top(jax.random.fold_in(splits[7], 71), 0)
    u_mid = gaussian(splits[1], (MIDS, NT, NM), NT ** -0.5, 0.125, ((0, 4), (1, 8)))
    b_mid = draw_b_mid(jax.random.fold_in(splits[7], 71), 0)
    u_leaf = gaussian(splits[3], (LEAVES, BORDER, LEAF_COLS), BORDER ** -0.5, 0.15625, ((0, 32),))
    leaf_index = draw_leaf_index(jax.random.fold_in(splits[7], 71), 0)
    leaf_count = draw_leaf_count(jax.random.fold_in(splits[7], 71), 0)
    leaf_bdiag = jnp.clip(4.0 + 12.0 * jax.random.uniform(splits[6], (LEAVES, LEAF_COLS), jnp.float32) ** levels(splits[6], (LEAVES, LEAF_COLS), ((0, 32),), -0.2, 0.2), 4.0, 16.0)
    return dict(g_top=g_top, u_mid=u_mid, b_mid=b_mid, u_leaf=u_leaf, leaf_index=leaf_index, leaf_count=leaf_count, leaf_bdiag=leaf_bdiag)


def reference(g_top, u_mid, b_mid, u_leaf, leaf_index, leaf_count, leaf_bdiag):
    def middle(operands):
        factor, inverse_block = operands
        cross_rows = (-jnp.dot(g_top, factor, preferred_element_type=jnp.float32)).astype(jnp.bfloat16)
        projected = jnp.dot(factor.T, cross_rows, preferred_element_type=jnp.float32)
        mid_rows = (inverse_block - projected).astype(jnp.bfloat16)
        return cross_rows, mid_rows

    mid_cross, mid_block = lax.map(middle, (u_mid, b_mid))

    def one_leaf(operands):
        owner_group, factor, slot_index, live_count, bdiagonal = operands
        cross_rows = mid_cross[owner_group]
        mid_rows = mid_block[owner_group]
        upper_rows = jnp.concatenate([g_top, cross_rows], axis=1)
        top_side = slot_index < NT
        clipped = jnp.minimum(slot_index, NT - 1).astype(jnp.int32)
        midpos = jnp.maximum(slot_index - NT, 0).astype(jnp.int32)
        picked = jnp.take(jnp.take(upper_rows, clipped, axis=0), slot_index, axis=1)
        mid_mid = jnp.take(jnp.take(mid_rows, midpos, axis=0), midpos, axis=1)
        chosen = jnp.where(top_side[:, None], picked, jnp.where(top_side[None, :], picked.T, mid_mid))
        live_slot = jnp.arange(BORDER, dtype=jnp.int32) < live_count
        masked = jnp.where(live_slot[:, None], factor, jnp.zeros((), factor.dtype))
        product = jnp.dot(chosen, masked, preferred_element_type=jnp.float32)
        offdiag = jnp.where(live_slot[:, None], -product, jnp.zeros((), jnp.float32)).astype(jnp.bfloat16)
        diagonal = bdiagonal + jnp.sum(masked.astype(jnp.float32) * product, axis=0)
        return offdiag, diagonal

    groups = (jnp.arange(LEAVES, dtype=jnp.int32) // N_SUB).astype(jnp.int32)
    leaf_offdiag, leaf_diag = lax.map(one_leaf, (groups, u_leaf, leaf_index, leaf_count, leaf_bdiag))
    return mid_cross, mid_block, leaf_offdiag, leaf_diag
```

```python
import functools
import math

import jax
import jax.numpy as jnp
from jax import lax
from jax.experimental import pallas as pl
from jax.experimental.pallas import tpu as pltpu
from jax.sharding import PartitionSpec as P

MESH = pl.DeviceIdType.MESH
F32 = jnp.float32
BF16 = jnp.bfloat16


def nearest(p, k, n):
    room = jnp.minimum(p, n - 1 - p)
    near = jnp.where(k % 2 == 1, p - (k + 1) // 2, p + k // 2)
    far = jnp.where(p < n - 1 - p, k, n - 1 - k)
    return jnp.where(k <= 2 * room, near, far)


def gather_kernel(nx, ny, nz, g_ref, u_ref, b_ref, g_all, u_all, b_all,
                  own_sem, g_recv, g_peer, g_send, u_recv, u_send, b_recv, b_send):
    sep, sub = lax.axis_index("sep"), lax.axis_index("sub")
    x, core = sep // 2, sep % 2
    z, y = sub // ny, sub % ny
    rows, cols = g_ref.shape
    mid = b_ref.shape[0]

    def device(xx, cc, zz, yy):
        return (xx * 2 + cc, zz * ny + yy)

    def g_block(zz, yy, xx, cc):
        return g_all.at[pl.ds(pl.multiple_of((zz * ny + yy) * rows, rows), rows),
                        pl.ds(pl.multiple_of((xx * 2 + cc) * cols, cols), cols)]

    def u_block(zz, yy):
        return u_all.at[pl.ds(pl.multiple_of((zz * ny + yy) * rows, rows), rows), :]

    def b_block(zz, yy):
        return b_all.at[pl.ds(pl.multiple_of((zz * ny + yy) * mid, mid), mid), :]

    steps = (
        (x > 0, device(x - 1, core, z, y)),
        (x < nx - 1, device(x + 1, core, z, y)),
        (y > 0, device(x, core, z, y - 1)),
        (y < ny - 1, device(x, core, z, y + 1)),
        (z > 0, device(x, core, z - 1, y)),
        (z < nz - 1, device(x, core, z + 1, y)),
        (core >= 0, device(x, 1 - core, z, y)),
    )
    own = (
        pltpu.make_async_copy(g_ref, g_block(z, y, x, core), own_sem.at[0]),
        pltpu.make_async_copy(u_ref, u_block(z, y), own_sem.at[1]),
        pltpu.make_async_copy(b_ref, b_block(z, y), own_sem.at[2]),
    )
    for copy in own:
        copy.start()
    barrier = pltpu.get_barrier_semaphore()
    total = jnp.int32(0)
    for valid, target in steps:
        total = total + valid.astype(jnp.int32)

        @pl.when(valid)
        def _():
            pl.semaphore_signal(barrier, inc=1, device_id=target, device_id_type=MESH)
    pl.semaphore_wait(barrier, total)
    for copy in own:
        copy.wait()

    def send(go, way, block, send_sem, recv_sem, start):
        valid, target = steps[way]

        @pl.when(jnp.logical_and(go, valid))
        def _():
            copy = pltpu.make_async_remote_copy(
                src_ref=block, dst_ref=block, send_sem=send_sem.at[way], recv_sem=recv_sem,
                device_id=target, device_id_type=MESH)
            if start:
                copy.start()
            else:
                copy.wait_send()

    def arrive(block, send_sem, recv_sem):
        pltpu.make_async_remote_copy(
            src_ref=block, dst_ref=block, send_sem=send_sem, recv_sem=recv_sem,
            device_id=steps[6][1], device_id_type=MESH).wait_recv()

    def g_event(zz, yy, xx, start):
        index = (zz * ny + yy) * nx + xx
        block = g_block(zz, yy, xx, core)
        sems = g_send.at[index]
        if start:
            @pl.when(jnp.logical_or(xx != x, jnp.logical_or(yy != y, zz != z)))
            def _():
                arrive(block, sems.at[0], g_recv.at[index])
        in_x = xx == x
        in_xy = jnp.logical_and(in_x, yy == y)
        go = functools.partial(send, block=block, send_sem=sems, recv_sem=g_recv.at[index], start=start)
        go(xx >= x, 0)
        go(xx <= x, 1)
        go(jnp.logical_and(in_x, yy >= y), 2)
        go(jnp.logical_and(in_x, yy <= y), 3)
        go(jnp.logical_and(in_xy, zz >= z), 4)
        go(jnp.logical_and(in_xy, zz <= z), 5)
        send(core >= 0, 6, block, sems, g_peer.at[index], start)

    def u_event(zz, yy, start):
        index = zz * ny + yy
        block = u_block(zz, yy)
        sems = u_send.at[index]
        if start:
            @pl.when(jnp.logical_or(yy != y, zz != z))
            def _():
                arrive(block, sems.at[0], u_recv.at[index])
        in_y = yy == y
        go = functools.partial(send, block=block, send_sem=sems, recv_sem=u_recv.at[index], start=start)
        go(yy >= y, 2)
        go(yy <= y, 3)
        go(jnp.logical_and(in_y, zz >= z), 4)
        go(jnp.logical_and(in_y, zz <= z), 5)

    def b_event(zz, yy, start):
        index = zz * ny + yy
        block = b_block(zz, yy)
        sems = b_send.at[index]
        if start:
            @pl.when(jnp.logical_or(yy != y, zz != z))
            def _():
                arrive(block, sems.at[0], b_recv.at[index])
        in_z = zz == z
        go = functools.partial(send, block=block, send_sem=sems, recv_sem=b_recv.at[index], start=start)
        go(jnp.logical_and(in_z, yy >= y), 2)
        go(jnp.logical_and(in_z, yy <= y), 3)
        go(zz >= z, 4)
        go(zz <= z, 5)

    def over_y(body):
        def run(k, carry):
            body(nearest(y, k, ny))
            return carry
        lax.fori_loop(0, ny, run, 0)

    def over_x(first, body):
        def run(k, carry):
            body(nearest(x, k, nx))
            return carry
        lax.fori_loop(first, nx, run, 0)

    def group(k, carry):
        @pl.when(k < nz)
        def _():
            zz = nearest(z, k, nz)
            over_y(lambda yy: g_event(zz, yy, x, True))
            over_y(lambda yy: u_event(zz, yy, True))
            over_y(lambda yy: b_event(zz, yy, True))

        @pl.when(k > 0)
        def _():
            zz = nearest(z, k - 1, nz)
            over_y(lambda yy: over_x(1, lambda xx: g_event(zz, yy, xx, True)))
        return carry

    lax.fori_loop(0, nz + 1, group, 0)

    def finish(zz, carry):
        def inner(yy, carry):
            u_event(zz, yy, False)
            b_event(zz, yy, False)

            def last(xx, carry):
                g_event(zz, yy, xx, False)
                index = (zz * ny + yy) * nx + xx
                arrive(g_block(zz, yy, xx, 1 - core), g_send.at[index].at[6], g_peer.at[index])
                return carry
            return lax.fori_loop(0, nx, last, carry)
        return lax.fori_loop(0, ny, inner, carry)

    lax.fori_loop(0, nz, finish, 0)


def gather_all(n_sep, n_sub, g_top, u_mid, b_mid):
    nx = n_sep // 2
    ny = math.isqrt(n_sub // 2)
    nz = n_sub // ny
    order = g_top.shape[0] * n_sub
    dma = pltpu.SemaphoreType.DMA
    n = nx * n_sub
    any_space = pl.BlockSpec(memory_space=pl.ANY)
    vmem = pl.BlockSpec(memory_space=pltpu.VMEM)
    return pl.pallas_call(
        functools.partial(gather_kernel, nx, ny, nz),
        out_shape=(
            jax.ShapeDtypeStruct((order, order), g_top.dtype),
            jax.ShapeDtypeStruct((order, u_mid.shape[1]), u_mid.dtype),
            jax.ShapeDtypeStruct((b_mid.shape[0] * n_sub, b_mid.shape[1]), b_mid.dtype),
        ),
        in_specs=[vmem] * 3,
        out_specs=(any_space,) * 3,
        scratch_shapes=[
            dma((3,)), dma((n,)), dma((n,)), dma((n, 7)),
            dma((n_sub,)), dma((n_sub, 7)), dma((n_sub,)), dma((n_sub, 7)),
        ],
        compiler_params=pltpu.CompilerParams(collective_id=0, has_side_effects=True),
    )(g_top, u_mid, b_mid)


def leaf_kernel(top, g_ref, cross_ref, cross_t_ref, mid_ref, across_ref, down_ref, bdiag_ref, u_ref,
                off_ref, diag_ref, pick, place):
    @pl.when(pl.program_id(0) == 0)
    def _():
        step = 256

        @pl.loop(0, place.shape[0] // step)
        def _(i):
            at = pl.multiple_of(i * step, step)
            row = lax.broadcasted_iota(jnp.int32, (step, place.shape[1]), 0) + at
            place[pl.ds(at, step), :] = jnp.where(row == across_ref[...], 1.0, 0.0).astype(BF16)

        @pl.loop(0, pick.shape[0] // step)
        def _(i):
            at = pl.multiple_of(i * step, step)
            column = lax.broadcasted_iota(jnp.int32, (step, pick.shape[1]), 1)
            pick[pl.ds(at, step), :] = jnp.where(column == down_ref[pl.ds(at, step), :], 1.0, 0.0).astype(BF16)

    dot = functools.partial(jnp.dot, preferred_element_type=F32)
    spread = dot(place[...], u_ref[...]).astype(BF16)
    upper, lower = spread[:top], spread[top:]
    high = dot(g_ref[...], upper) + dot(cross_ref[...], lower)
    low = dot(cross_t_ref[...], upper) + dot(mid_ref[...], lower)
    diag_ref[...] = (bdiag_ref[...]
                     + jnp.sum(upper.astype(F32) * high, axis=0, keepdims=True)
                     + jnp.sum(lower.astype(F32) * low, axis=0, keepdims=True))
    picked = dot(pick[:, :top], (-high).astype(BF16)) + dot(pick[:, top:], (-low).astype(BF16))
    off_ref[...] = picked.astype(BF16)


def leaf(g_all, cross, mid, slot_index, u_leaf, bdiag):
    top, wide = cross.shape
    slots, columns = u_leaf.shape
    total = top + wide
    tile = 256
    once = pl.Buffered(1)

    def whole(shape):
        return pl.BlockSpec(shape, lambda j: (0,) * len(shape), pipeline_mode=once)
    return pl.pallas_call(
        functools.partial(leaf_kernel, top),
        grid=(columns // tile,),
        out_shape=(jax.ShapeDtypeStruct((slots, columns), BF16),
                   jax.ShapeDtypeStruct((1, columns), F32)),
        in_specs=[
            whole((top, top)), whole((top, wide)), whole((wide, top)), whole((wide, wide)),
            whole((1, slots)), whole((slots, 1)),
            pl.BlockSpec((1, tile), lambda j: (0, j)),
            pl.BlockSpec((slots, tile), lambda j: (0, j)),
        ],
        out_specs=(pl.BlockSpec((slots, tile), lambda j: (0, j)),
                   pl.BlockSpec((1, tile), lambda j: (0, j))),
        scratch_shapes=[pltpu.VMEM((slots, total), BF16), pltpu.VMEM((total, slots), BF16)],
        compiler_params=pltpu.CompilerParams(vmem_limit_bytes=60 * 2**20),
    )(g_all, cross, cross.T, mid, slot_index[None, :], slot_index[:, None], bdiag[None, :], u_leaf)


def shards(n_sep, n_sub, g_top, u_mid, b_mid, u_leaf, leaf_index, leaf_count, leaf_bdiag):
    rows, mid = u_mid.shape[1], b_mid.shape[1]
    g_all, u_all, b_all = gather_all(n_sep, n_sub, g_top, u_mid[0], b_mid[0])
    cross = (-jnp.dot(g_all, u_all, preferred_element_type=F32)).astype(BF16)
    projected = lax.dot_general(u_all, cross, (((0,), (0,)), ((), ())), preferred_element_type=F32)
    block = (b_all - projected).astype(BF16)
    me = lax.axis_index("sub")
    cross_rows = lax.dynamic_slice_in_dim(cross, me * rows, rows, 0)
    mid_rows = lax.dynamic_slice_in_dim(block, me * mid, mid, 0)
    slots = leaf_index.shape[1]
    live = jnp.arange(slots, dtype=jnp.int32) < leaf_count[0]
    slot_index = jnp.where(live, leaf_index[0], -1)
    off, diag = leaf(g_all, cross, block, slot_index, u_leaf[0], leaf_bdiag[0])
    return cross_rows[None], mid_rows[None], off[None], diag


def solution(mesh):
    return jax.shard_map(
        functools.partial(shards, mesh.shape["sep"], mesh.shape["sub"]),
        mesh=mesh,
        in_specs=(
            P("sub", "sep"),
            P("sep", "sub", None),
            P("sep", "sub", None),
            P(("sep", "sub"), None, None),
            P(("sep", "sub"), None),
            P(("sep", "sub")),
            P(("sep", "sub"), None),
        ),
        out_specs=(
            P("sep", "sub", None),
            P("sep", "sub", None),
            P(("sep", "sub"), None, None),
            P(("sep", "sub"), None),
        ),
        check_vma=False,
    )
```

```python
import functools
import math

import jax
import jax.numpy as jnp
from jax import lax
from jax.experimental import pallas as pl
from jax.experimental.pallas import tpu as pltpu
from jax.sharding import PartitionSpec as P

MESH = pl.DeviceIdType.MESH
F32 = jnp.float32
BF16 = jnp.bfloat16


def nearest(p, k, n):
    room = jnp.minimum(p, n - 1 - p)
    near = jnp.where(k % 2 == 1, p - (k + 1) // 2, p + k // 2)
    far = jnp.where(p < n - 1 - p, k, n - 1 - k)
    return jnp.where(k <= 2 * room, near, far)


def gather_kernel(nx, ny, nz, g_ref, u_ref, b_ref, across_ref, bdiag_ref, leaf_ref,
                  cross_out, mid_out, y_ref, diag_ref,
                  g_all, u_all, b_all, leaf_all, spread, low, projected, block,
                  own_sem, g_recv, g_peer, g_send, u_recv, u_send, b_recv, b_send):
    sep, sub = lax.axis_index("sep"), lax.axis_index("sub")
    x, core = sep // 2, sep % 2
    z, y = sub // ny, sub % ny
    rows, cols = g_ref.shape
    mid = b_ref.shape[0]

    def device(xx, cc, zz, yy):
        return (xx * 2 + cc, zz * ny + yy)

    def g_block(zz, yy, xx, cc):
        return g_all.at[pl.ds(pl.multiple_of((zz * ny + yy) * rows, rows), rows),
                        pl.ds(pl.multiple_of((xx * 2 + cc) * cols, cols), cols)]

    def u_block(zz, yy):
        return u_all.at[pl.ds(pl.multiple_of((zz * ny + yy) * rows, rows), rows), :]

    def b_block(zz, yy):
        return b_all.at[pl.ds(pl.multiple_of((zz * ny + yy) * mid, mid), mid), :]

    steps = (
        (x > 0, device(x - 1, core, z, y)),
        (x < nx - 1, device(x + 1, core, z, y)),
        (y > 0, device(x, core, z, y - 1)),
        (y < ny - 1, device(x, core, z, y + 1)),
        (z > 0, device(x, core, z - 1, y)),
        (z < nz - 1, device(x, core, z + 1, y)),
        (core >= 0, device(x, 1 - core, z, y)),
    )
    own = (
        pltpu.make_async_copy(g_ref, g_block(z, y, x, core), own_sem.at[0]),
        pltpu.make_async_copy(u_ref, u_block(z, y), own_sem.at[1]),
        pltpu.make_async_copy(b_ref, b_block(z, y), own_sem.at[2]),
    )
    leaf_copy = pltpu.make_async_copy(leaf_ref, leaf_all, own_sem.at[3])
    for copy in own:
        copy.start()
    leaf_copy.start()
    barrier = pltpu.get_barrier_semaphore()
    total = jnp.int32(0)
    for valid, target in steps:
        total = total + valid.astype(jnp.int32)

        @pl.when(valid)
        def _():
            pl.semaphore_signal(barrier, inc=1, device_id=target, device_id_type=MESH)
    pl.semaphore_wait(barrier, total)
    for copy in own:
        copy.wait()

    def send(go, way, block, send_sem, recv_sem, start):
        valid, target = steps[way]

        @pl.when(jnp.logical_and(go, valid))
        def _():
            copy = pltpu.make_async_remote_copy(
                src_ref=block, dst_ref=block, send_sem=send_sem.at[way], recv_sem=recv_sem,
                device_id=target, device_id_type=MESH)
            if start:
                copy.start()
            else:
                copy.wait_send()

    def arrive(block, send_sem, recv_sem):
        pltpu.make_async_remote_copy(
            src_ref=block, dst_ref=block, send_sem=send_sem, recv_sem=recv_sem,
            device_id=steps[6][1], device_id_type=MESH).wait_recv()

    def g_event(zz, yy, xx, start):
        index = (zz * ny + yy) * nx + xx
        block = g_block(zz, yy, xx, core)
        sems = g_send.at[index]
        if start:
            @pl.when(jnp.logical_or(xx != x, jnp.logical_or(yy != y, zz != z)))
            def _():
                arrive(block, sems.at[0], g_recv.at[index])
        in_x = xx == x
        in_xy = jnp.logical_and(in_x, yy == y)
        go = functools.partial(send, block=block, send_sem=sems, recv_sem=g_recv.at[index], start=start)
        go(xx >= x, 0)
        go(xx <= x, 1)
        go(jnp.logical_and(in_x, yy >= y), 2)
        go(jnp.logical_and(in_x, yy <= y), 3)
        go(jnp.logical_and(in_xy, zz >= z), 4)
        go(jnp.logical_and(in_xy, zz <= z), 5)
        send(core >= 0, 6, block, sems, g_peer.at[index], start)

    def u_event(zz, yy, start):
        index = zz * ny + yy
        block = u_block(zz, yy)
        sems = u_send.at[index]
        if start:
            @pl.when(jnp.logical_or(yy != y, zz != z))
            def _():
                arrive(block, sems.at[0], u_recv.at[index])
        in_y = yy == y
        go = functools.partial(send, block=block, send_sem=sems, recv_sem=u_recv.at[index], start=start)
        go(yy >= y, 2)
        go(yy <= y, 3)
        go(jnp.logical_and(in_y, zz >= z), 4)
        go(jnp.logical_and(in_y, zz <= z), 5)

    def b_event(zz, yy, start):
        index = zz * ny + yy
        block = b_block(zz, yy)
        sems = b_send.at[index]
        if start:
            @pl.when(jnp.logical_or(yy != y, zz != z))
            def _():
                arrive(block, sems.at[0], b_recv.at[index])
        in_z = zz == z
        go = functools.partial(send, block=block, send_sem=sems, recv_sem=b_recv.at[index], start=start)
        go(jnp.logical_and(in_z, yy >= y), 2)
        go(jnp.logical_and(in_z, yy <= y), 3)
        go(zz >= z, 4)
        go(zz <= z, 5)

    def over_y(body):
        def run(k, carry):
            body(nearest(y, k, ny))
            return carry
        lax.fori_loop(0, ny, run, 0)

    def over_x(first, body):
        def run(k, carry):
            body(nearest(x, k, nx))
            return carry
        lax.fori_loop(first, nx, run, 0)

    top, wide = u_all.shape
    chunk = 256
    half = spread.shape[0] // chunk // 2
    tile = 512
    dot = functools.partial(jnp.dot, preferred_element_type=F32)
    dot_t = functools.partial(lax.dot_general, dimension_numbers=(((0,), (0,)), ((), ())),
                              preferred_element_type=F32)

    def place(first, last):
        @pl.loop(first, last)
        def _(i):
            at = pl.multiple_of(i * chunk, chunk)
            row = lax.broadcasted_iota(jnp.int32, (chunk, across_ref.shape[1]), 0) + at
            one_hot = jnp.where(row == across_ref[...], 1.0, 0.0).astype(BF16)
            spread[pl.ds(at, chunk), :] = dot(one_hot, leaf_all[...]).astype(BF16)

    def add_diag(part, product, span):
        diag_ref[:, span] += jnp.sum(part.astype(F32) * product, axis=0, keepdims=True)

    def compute(zz, yy):
        at = pl.ds(pl.multiple_of((zz * ny + yy) * rows, rows), rows)
        cross = (-dot(g_all[at, :], u_all[...])).astype(BF16)

        @pl.when(jnp.logical_and(zz == z, yy == y))
        def _():
            cross_out[...] = cross
        projected[...] += dot_t(u_all[at, :], cross)

        @pl.loop(0, y_ref.shape[1] // tile)
        def _(j):
            span = pl.ds(pl.multiple_of(j * tile, tile), tile)
            own_part = spread[at, span]
            product = dot(g_all[at, :], spread[:top, span]) + dot(cross, spread[top:, span])
            y_ref[at, span] = (-product).astype(BF16)
            add_diag(own_part, product, span)
            low[:, span] += dot_t(cross, own_part)

    projected[...] = jnp.zeros_like(projected)
    low[...] = jnp.zeros_like(low)
    diag_ref[...] = bdiag_ref[...]

    def group(k, carry):
        @pl.when(k < nz)
        def _():
            zz = nearest(z, k, nz)
            over_y(lambda yy: g_event(zz, yy, x, True))

        @pl.when(k == 0)
        def _():
            over_y(lambda yy: u_event(nearest(z, 0, nz), yy, True))
            leaf_copy.wait()
            place(0, half)
            over_y(lambda yy: u_event(nearest(z, 1, nz), yy, True))

        @pl.when(k == 1)
        def _():
            over_y(lambda yy: u_event(nearest(z, 2, nz), yy, True))
            place(half, 2 * half)

            def rest(i, carry):
                over_y(lambda yy: u_event(nearest(z, i, nz), yy, True))
                return carry
            lax.fori_loop(3, nz, rest, 0)

        @pl.when(k < nz)
        def _():
            over_y(lambda yy: b_event(nearest(z, k, nz), yy, True))

        @pl.when(k > 1)
        def _():
            zz = nearest(z, k - 2, nz)

            def rows_of(yy):
                def peer(xx, carry):
                    index = (zz * ny + yy) * nx + xx
                    arrive(g_block(zz, yy, xx, 1 - core), g_send.at[index].at[6], g_peer.at[index])
                    return carry
                lax.fori_loop(0, nx, peer, 0)
                compute(zz, yy)
            over_y(rows_of)

        @pl.when(jnp.logical_and(k > 0, k <= nz))
        def _():
            zz = nearest(z, k - 1, nz)
            over_y(lambda yy: over_x(1, lambda xx: g_event(zz, yy, xx, True)))
        return carry

    lax.fori_loop(0, nz + 2, group, 0)

    block[...] = (b_all[...] - projected[...]).astype(BF16)
    mid_out[...] = block[pl.ds(pl.multiple_of((z * ny + y) * mid, mid), mid), :]

    @pl.loop(0, y_ref.shape[1] // tile)
    def _(j):
        span = pl.ds(pl.multiple_of(j * tile, tile), tile)
        part = spread[top:, span]
        product = low[:, span] + dot(block[...], part)
        y_ref[top:, span] = (-product).astype(BF16)
        add_diag(part, product, span)

    def finish(zz, carry):
        def inner(yy, carry):
            u_event(zz, yy, False)
            b_event(zz, yy, False)

            def last(xx, carry):
                g_event(zz, yy, xx, False)
                return carry
            return lax.fori_loop(0, nx, last, carry)
        return lax.fori_loop(0, ny, inner, carry)

    lax.fori_loop(0, nz, finish, 0)


def gather_all(n_sep, n_sub, g_top, u_mid, b_mid, across, bdiag, u_leaf):
    nx = n_sep // 2
    ny = math.isqrt(n_sub // 2)
    nz = n_sub // ny
    top = g_top.shape[0] * n_sub
    wide = u_mid.shape[1]
    slots, columns = u_leaf.shape
    dma = pltpu.SemaphoreType.DMA
    n = nx * n_sub
    any_space = pl.BlockSpec(memory_space=pl.ANY)
    vmem = pl.BlockSpec(memory_space=pltpu.VMEM)
    return pl.pallas_call(
        functools.partial(gather_kernel, nx, ny, nz),
        out_shape=(
            jax.ShapeDtypeStruct(u_mid.shape, BF16),
            jax.ShapeDtypeStruct(b_mid.shape, BF16),
            jax.ShapeDtypeStruct((top + wide, columns), BF16),
            jax.ShapeDtypeStruct((1, columns), F32),
        ),
        in_specs=[any_space] * 3 + [vmem] * 2 + [any_space],
        out_specs=(vmem,) * 4,
        scratch_shapes=[
            pltpu.VMEM((top, top), BF16), pltpu.VMEM((top, wide), BF16), pltpu.VMEM((wide, wide), F32),
            pltpu.VMEM((slots, columns), BF16), pltpu.VMEM((top + wide, columns), BF16),
            pltpu.VMEM((wide, columns), F32), pltpu.VMEM((wide, wide), F32), pltpu.VMEM((wide, wide), BF16),
            dma((4,)), dma((n,)), dma((n,)), dma((n, 7)),
            dma((n_sub,)), dma((n_sub, 7)), dma((n_sub,)), dma((n_sub, 7)),
        ],
        compiler_params=pltpu.CompilerParams(collective_id=0, has_side_effects=True,
                                             vmem_limit_bytes=60 * 2**20),
    )(g_top, u_mid, b_mid, across, bdiag, u_leaf)


def pick_kernel(down_ref, y_ref, off_ref):
    column = lax.broadcasted_iota(jnp.int32, (off_ref.shape[0], y_ref.shape[0]), 1)
    pick = jnp.where(column == down_ref[...], 1.0, 0.0).astype(BF16)
    off_ref[...] = jnp.dot(pick, y_ref[...], preferred_element_type=F32).astype(BF16)


def pick_rows(down, y):
    slots, (total, columns) = down.shape[0], y.shape
    tile = 256
    return pl.pallas_call(
        pick_kernel,
        grid=(slots // tile,),
        out_shape=jax.ShapeDtypeStruct((slots, columns), BF16),
        in_specs=[
            pl.BlockSpec((tile, 1), lambda i: (i, 0)),
            pl.BlockSpec((total, columns), lambda i: (0, 0), pipeline_mode=pl.Buffered(1)),
        ],
        out_specs=pl.BlockSpec((tile, columns), lambda i: (i, 0)),
        compiler_params=pltpu.CompilerParams(vmem_limit_bytes=40 * 2**20),
    )(down, y)


def shards(n_sep, n_sub, g_top, u_mid, b_mid, u_leaf, leaf_index, leaf_count, leaf_bdiag):
    slots = leaf_index.shape[1]
    live = jnp.arange(slots, dtype=jnp.int32)[None, :] < leaf_count[0]
    across = jnp.where(live, leaf_index, -1)
    cross_rows, mid_rows, y, diag = gather_all(
        n_sep, n_sub, g_top, u_mid[0], b_mid[0], across, leaf_bdiag, u_leaf[0])
    off = pick_rows(across.reshape(slots, 1), y)
    return cross_rows[None], mid_rows[None], off[None], diag


def solution(mesh):
    return jax.shard_map(
        functools.partial(shards, mesh.shape["sep"], mesh.shape["sub"]),
        mesh=mesh,
        in_specs=(
            P("sub", "sep"),
            P("sep", "sub", None),
            P("sep", "sub", None),
            P(("sep", "sub"), None, None),
            P(("sep", "sub"), None),
            P(("sep", "sub")),
            P(("sep", "sub"), None),
        ),
        out_specs=(
            P("sep", "sub", None),
            P("sep", "sub", None),
            P(("sep", "sub"), None, None),
            P(("sep", "sub"), None),
        ),
        check_vma=False,
    )
```

```python
import functools
import math

import jax
import jax.numpy as jnp
from jax import lax
from jax.experimental import pallas as pl
from jax.experimental.pallas import tpu as pltpu
from jax.sharding import PartitionSpec as P

MESH = pl.DeviceIdType.MESH
F32 = jnp.float32
BF16 = jnp.bfloat16


def nearest(p, k, n):
    room = jnp.minimum(p, n - 1 - p)
    near = jnp.where(k % 2 == 1, p - (k + 1) // 2, p + k // 2)
    far = jnp.where(p < n - 1 - p, k, n - 1 - k)
    return jnp.where(k <= 2 * room, near, far)


def gather_kernel(nx, ny, nz, g_ref, u_ref, b_ref, across_ref, bdiag_ref, leaf_ref,
                  cross_out, mid_out, y_ref, diag_ref,
                  g_all, u_all, b_all, leaf_all, spread, low, projected, block, crossed,
                  own_sem, z_send, g_recv, g_peer, g_send, u_recv, u_send, b_recv, b_send):
    sep, sub = lax.axis_index("sep"), lax.axis_index("sub")
    x, core = sep // 2, sep % 2
    z, y = sub // ny, sub % ny
    rows, cols = g_ref.shape
    mid = b_ref.shape[0]

    def device(xx, cc, zz, yy):
        return (xx * 2 + cc, zz * ny + yy)

    def g_block(zz, yy, xx, cc):
        return g_all.at[pl.ds(pl.multiple_of((zz * ny + yy) * rows, rows), rows),
                        pl.ds(pl.multiple_of((xx * 2 + cc) * cols, cols), cols)]

    def u_block(zz, yy):
        return u_all.at[pl.ds(pl.multiple_of((zz * ny + yy) * rows, rows), rows), :]

    def b_block(zz, yy):
        return b_all.at[pl.ds(pl.multiple_of((zz * ny + yy) * mid, mid), mid), :]

    steps = (
        (x > 0, device(x - 1, core, z, y)),
        (x < nx - 1, device(x + 1, core, z, y)),
        (y > 0, device(x, core, z, y - 1)),
        (y < ny - 1, device(x, core, z, y + 1)),
        (core >= 0, device(x, 1 - core, z, y)),
    )
    own = (
        pltpu.make_async_copy(g_ref, g_block(z, y, x, core), own_sem.at[0]),
        pltpu.make_async_copy(u_ref, u_block(z, y), own_sem.at[1]),
        pltpu.make_async_copy(b_ref, b_block(z, y), own_sem.at[2]),
    )
    leaf_copy = pltpu.make_async_copy(leaf_ref, leaf_all, own_sem.at[3])
    for copy in own:
        copy.start()
    leaf_copy.start()
    barrier = pltpu.get_barrier_semaphore()
    total = jnp.int32(nz - 1)

    def greet(j, carry):
        pl.semaphore_signal(barrier, inc=1, device_id=device(x, core, nearest(z, j, nz), y), device_id_type=MESH)
        return carry
    lax.fori_loop(1, nz, greet, 0)
    for valid, target in steps:
        total = total + valid.astype(jnp.int32)

        @pl.when(valid)
        def _():
            pl.semaphore_signal(barrier, inc=1, device_id=target, device_id_type=MESH)
    pl.semaphore_wait(barrier, total)
    for copy in own:
        copy.wait()

    def send(go, way, block, send_sem, recv_sem, start):
        valid, target = steps[way]

        @pl.when(jnp.logical_and(go, valid))
        def _():
            copy = pltpu.make_async_remote_copy(
                src_ref=block, dst_ref=block, send_sem=send_sem.at[way], recv_sem=recv_sem,
                device_id=target, device_id_type=MESH)
            if start:
                copy.start()
            else:
                copy.wait_send()

    def arrive(block, send_sem, recv_sem):
        pltpu.make_async_remote_copy(
            src_ref=block, dst_ref=block, send_sem=send_sem, recv_sem=recv_sem,
            device_id=steps[4][1], device_id_type=MESH).wait_recv()

    me = z * ny + y
    own_blocks = (
        (g_block(z, y, x, core), g_recv.at[me * nx + x]),
        (u_block(z, y), u_recv.at[me]),
        (b_block(z, y), b_recv.at[me]),
    )

    def column(which, start, near=None):
        block, recv_sem = own_blocks[which]

        def one(j, carry):
            zz = nearest(z, j, nz)
            beside = jnp.logical_or(zz == z - 1, zz == z + 1)
            wanted = zz >= 0 if near is None else beside if near else jnp.logical_not(beside)

            @pl.when(wanted)
            def _():
                copy = pltpu.make_async_remote_copy(
                    src_ref=block, dst_ref=block, send_sem=z_send.at[which, zz], recv_sem=recv_sem,
                    device_id=device(x, core, zz, y), device_id_type=MESH)
                if start:
                    copy.start()
                else:
                    copy.wait_send()
            return carry
        lax.fori_loop(1, nz, one, 0)

    def g_event(zz, yy, xx, start):
        index = (zz * ny + yy) * nx + xx
        block = g_block(zz, yy, xx, core)
        sems = g_send.at[index]
        if start:
            @pl.when(jnp.logical_or(xx != x, jnp.logical_or(yy != y, zz != z)))
            def _():
                arrive(block, sems.at[0], g_recv.at[index])
        in_x = xx == x
        go = functools.partial(send, block=block, send_sem=sems, recv_sem=g_recv.at[index], start=start)
        go(jnp.logical_and(in_x, yy >= y), 2)
        go(jnp.logical_and(in_x, yy <= y), 3)
        go(xx >= x, 0)
        go(xx <= x, 1)
        send(core >= 0, 4, block, sems, g_peer.at[index], start)

    def flat_event(view, send_sems, recv_sems, zz, yy, start):
        index = zz * ny + yy
        block = view(zz, yy)
        sems = send_sems.at[index]
        if start:
            @pl.when(jnp.logical_or(yy != y, zz != z))
            def _():
                arrive(block, sems.at[0], recv_sems.at[index])
        send(yy >= y, 2, block, sems, recv_sems.at[index], start)
        send(yy <= y, 3, block, sems, recv_sems.at[index], start)

    u_event = functools.partial(flat_event, u_block, u_send, u_recv)
    b_event = functools.partial(flat_event, b_block, b_send, b_recv)

    def over_y(body, first=0):
        def run(k, carry):
            body(nearest(y, k, ny))
            return carry
        lax.fori_loop(first, ny, run, 0)

    def over_x(first, body):
        def run(k, carry):
            body(nearest(x, k, nx))
            return carry
        lax.fori_loop(first, nx, run, 0)

    top, wide = u_all.shape
    chunk = 256
    pieces = spread.shape[0] // chunk
    deep = ny * rows
    tile = 512
    dot = functools.partial(jnp.dot, preferred_element_type=F32)
    dot_t = functools.partial(lax.dot_general, dimension_numbers=(((0,), (0,)), ((), ())),
                              preferred_element_type=F32)

    def place(first, last):
        @pl.loop(first, last)
        def _(i):
            at = pl.multiple_of(i * chunk, chunk)
            row = lax.broadcasted_iota(jnp.int32, (chunk, across_ref.shape[1]), 0) + at
            one_hot = jnp.where(row == across_ref[...], 1.0, 0.0).astype(BF16)
            spread[pl.ds(at, chunk), :] = dot(one_hot, leaf_all[...]).astype(BF16)

    def add_diag(part, product, span):
        diag_ref[:, span] += jnp.sum(part.astype(F32) * product, axis=0, keepdims=True)

    def compute(zz):
        at = pl.ds(pl.multiple_of(zz * deep, deep), deep)
        cross = (-dot(g_all[at, :], u_all[...])).astype(BF16)

        @pl.when(zz == z)
        def _():
            crossed[...] = cross
            cross_out[...] = crossed[pl.ds(pl.multiple_of(y * rows, rows), rows), :]
        projected[...] += dot_t(u_all[at, :], cross)

        @pl.loop(0, y_ref.shape[1] // tile)
        def _(j):
            span = pl.ds(pl.multiple_of(j * tile, tile), tile)
            own_part = spread[at, span]
            product = dot(g_all[at, :], spread[:top, span]) + dot(cross, spread[top:, span])
            y_ref[at, span] = (-product).astype(BF16)
            add_diag(own_part, product, span)
            low[:, span] += dot_t(cross, own_part)

    projected[...] = jnp.zeros_like(projected)
    low[...] = jnp.zeros_like(low)
    diag_ref[...] = bdiag_ref[...]

    def cut(i):
        return pieces * i // (nz + 2)

    def g_group(k):
        zz = nearest(z, k, nz)
        over_y(lambda yy: g_event(zz, yy, x, True))

    def x_group(k):
        zz = nearest(z, k, nz)
        over_y(lambda yy: over_x(1, lambda xx: g_event(zz, yy, xx, True)))

    def b_group(k):
        zz = nearest(z, k, nz)
        over_y(lambda yy: b_event(zz, yy, True))

    column(0, True, True)
    g_event(z, y, x, True)
    column(1, True)
    u_event(z, y, True)
    column(0, True, False)
    column(2, True)
    leaf_copy.wait()
    place(0, cut(1))
    over_y(lambda yy: g_event(z, yy, x, True), 1)
    place(cut(1), cut(2))
    g_group(1)
    over_y(lambda yy: u_event(z, yy, True), 1)
    place(cut(2), cut(3))

    def u_group(k, carry):
        zz = nearest(z, k, nz)
        over_y(lambda yy: u_event(zz, yy, True))
        place(cut(k + 2), cut(k + 3))
        return carry
    lax.fori_loop(1, nz, u_group, 0)
    x_group(0)

    def group(k, carry):
        @pl.when(k < nz)
        def _():
            g_group(k)

        zz = nearest(z, k - 2, nz)

        def rows_of(yy):
            def peer(xx, carry):
                index = (zz * ny + yy) * nx + xx
                arrive(g_block(zz, yy, xx, 1 - core), g_send.at[index].at[4], g_peer.at[index])
                return carry
            lax.fori_loop(0, nx, peer, 0)
        over_y(rows_of)
        compute(zz)

        @pl.when(k == 2)
        def _():
            b_group(0)
            b_group(1)

        @pl.when(k < nz)
        def _():
            b_group(k)

        @pl.when(k <= nz)
        def _():
            x_group(k - 1)
        return carry

    lax.fori_loop(2, nz + 2, group, 0)

    block[...] = (b_all[...] - projected[...]).astype(BF16)
    mid_out[...] = block[pl.ds(pl.multiple_of((z * ny + y) * mid, mid), mid), :]

    @pl.loop(0, y_ref.shape[1] // tile)
    def _(j):
        span = pl.ds(pl.multiple_of(j * tile, tile), tile)
        part = spread[top:, span]
        product = low[:, span] + dot(block[...], part)
        y_ref[top:, span] = (-product).astype(BF16)
        add_diag(part, product, span)

    for which in range(3):
        column(which, False)

    def finish(zz, carry):
        def inner(yy, carry):
            u_event(zz, yy, False)
            b_event(zz, yy, False)

            def last(xx, carry):
                g_event(zz, yy, xx, False)
                return carry
            return lax.fori_loop(0, nx, last, carry)
        return lax.fori_loop(0, ny, inner, carry)

    lax.fori_loop(0, nz, finish, 0)


def gather_all(n_sep, n_sub, g_top, u_mid, b_mid, across, bdiag, u_leaf):
    nx = n_sep // 2
    ny = math.isqrt(n_sub // 2)
    nz = n_sub // ny
    top = g_top.shape[0] * n_sub
    wide = u_mid.shape[1]
    slots, columns = u_leaf.shape
    dma = pltpu.SemaphoreType.DMA
    n = nx * n_sub
    any_space = pl.BlockSpec(memory_space=pl.ANY)
    vmem = pl.BlockSpec(memory_space=pltpu.VMEM)
    return pl.pallas_call(
        functools.partial(gather_kernel, nx, ny, nz),
        out_shape=(
            jax.ShapeDtypeStruct(u_mid.shape, BF16),
            jax.ShapeDtypeStruct(b_mid.shape, BF16),
            jax.ShapeDtypeStruct((top + wide, columns), BF16),
            jax.ShapeDtypeStruct((1, columns), F32),
        ),
        in_specs=[any_space] * 3 + [vmem] * 2 + [any_space],
        out_specs=(vmem,) * 4,
        scratch_shapes=[
            pltpu.VMEM((top, top), BF16), pltpu.VMEM((top, wide), BF16), pltpu.VMEM((wide, wide), F32),
            pltpu.VMEM((slots, columns), BF16), pltpu.VMEM((top + wide, columns), BF16),
            pltpu.VMEM((wide, columns), F32), pltpu.VMEM((wide, wide), F32), pltpu.VMEM((wide, wide), BF16),
            pltpu.VMEM((top // nz, wide), BF16),
            dma((4,)), dma((3, nz)), dma((n,)), dma((n,)), dma((n, 5)),
            dma((n_sub,)), dma((n_sub, 5)), dma((n_sub,)), dma((n_sub, 5)),
        ],
        compiler_params=pltpu.CompilerParams(collective_id=0, has_side_effects=True,
                                             vmem_limit_bytes=60 * 2**20),
    )(g_top, u_mid, b_mid, across, bdiag, u_leaf)


def pick_kernel(down_ref, y_ref, off_ref):
    column = lax.broadcasted_iota(jnp.int32, (off_ref.shape[0], y_ref.shape[0]), 1)
    pick = jnp.where(column == down_ref[...], 1.0, 0.0).astype(BF16)
    off_ref[...] = jnp.dot(pick, y_ref[...], preferred_element_type=F32).astype(BF16)


def pick_rows(down, y):
    slots, (total, columns) = down.shape[0], y.shape
    tile = 256
    return pl.pallas_call(
        pick_kernel,
        grid=(slots // tile,),
        out_shape=jax.ShapeDtypeStruct((slots, columns), BF16),
        in_specs=[
            pl.BlockSpec((tile, 1), lambda i: (i, 0)),
            pl.BlockSpec((total, columns), lambda i: (0, 0), pipeline_mode=pl.Buffered(1)),
        ],
        out_specs=pl.BlockSpec((tile, columns), lambda i: (i, 0)),
        compiler_params=pltpu.CompilerParams(vmem_limit_bytes=40 * 2**20),
    )(down, y)


def shards(n_sep, n_sub, g_top, u_mid, b_mid, u_leaf, leaf_index, leaf_count, leaf_bdiag):
    slots = leaf_index.shape[1]
    live = jnp.arange(slots, dtype=jnp.int32)[None, :] < leaf_count[0]
    across = jnp.where(live, leaf_index, -1)
    cross_rows, mid_rows, y, diag = gather_all(
        n_sep, n_sub, g_top, u_mid[0], b_mid[0], across, leaf_bdiag, u_leaf[0])
    off = pick_rows(across.reshape(slots, 1), y)
    return cross_rows[None], mid_rows[None], off[None], diag


def solution(mesh):
    return jax.shard_map(
        functools.partial(shards, mesh.shape["sep"], mesh.shape["sub"]),
        mesh=mesh,
        in_specs=(
            P("sub", "sep"),
            P("sep", "sub", None),
            P("sep", "sub", None),
            P(("sep", "sub"), None, None),
            P(("sep", "sub"), None),
            P(("sep", "sub")),
            P(("sep", "sub"), None),
        ),
        out_specs=(
            P("sep", "sub", None),
            P("sep", "sub", None),
            P(("sep", "sub"), None, None),
            P(("sep", "sub"), None),
        ),
        check_vma=False,
    )
```

```python
import functools
import math

import jax
import jax.numpy as jnp
from jax import lax
from jax.experimental import pallas as pl
from jax.experimental.pallas import tpu as pltpu
from jax.sharding import PartitionSpec as P

MESH = pl.DeviceIdType.MESH
F32 = jnp.float32
BF16 = jnp.bfloat16


def nearest(p, k, n):
    room = jnp.minimum(p, n - 1 - p)
    near = jnp.where(k % 2 == 1, p - (k + 1) // 2, p + k // 2)
    far = jnp.where(p < n - 1 - p, k, n - 1 - k)
    return jnp.where(k <= 2 * room, near, far)


def gather_kernel(nx, ny, nz, g_ref, u_ref, b_ref, across_ref, bdiag_ref, leaf_ref, exact_ref,
                  cross_out, mid_out, y_ref, diag_ref,
                  g_all, u_all, b_all, leaf_all, spread, low, projected, block,
                  own_sem, g_recv, g_peer, g_send, u_recv, u_send, b_recv, b_send):
    sep, sub = lax.axis_index("sep"), lax.axis_index("sub")
    x, core = sep // 2, sep % 2
    z, y = sub // ny, sub % ny
    rows, cols = g_ref.shape
    mid = b_ref.shape[0]

    def device(xx, cc, zz, yy):
        return (xx * 2 + cc, zz * ny + yy)

    def g_block(zz, yy, xx, cc):
        return g_all.at[pl.ds(pl.multiple_of((zz * ny + yy) * rows, rows), rows),
                        pl.ds(pl.multiple_of((xx * 2 + cc) * cols, cols), cols)]

    def u_block(zz, yy):
        return u_all.at[pl.ds(pl.multiple_of((zz * ny + yy) * rows, rows), rows), :]

    def b_block(zz, yy):
        return b_all.at[pl.ds(pl.multiple_of((zz * ny + yy) * mid, mid), mid), :]

    steps = (
        (x > 0, device(x - 1, core, z, y)),
        (x < nx - 1, device(x + 1, core, z, y)),
        (y > 0, device(x, core, z, y - 1)),
        (y < ny - 1, device(x, core, z, y + 1)),
        (z > 0, device(x, core, z - 1, y)),
        (z < nz - 1, device(x, core, z + 1, y)),
        (core >= 0, device(x, 1 - core, z, y)),
    )
    own = (
        pltpu.make_async_copy(g_ref, g_block(z, y, x, core), own_sem.at[0]),
        pltpu.make_async_copy(u_ref, u_block(z, y), own_sem.at[1]),
        pltpu.make_async_copy(b_ref, b_block(z, y), own_sem.at[2]),
    )
    leaf_copy = pltpu.make_async_copy(leaf_ref, leaf_all, own_sem.at[3])
    for copy in own:
        copy.start()
    leaf_copy.start()
    barrier = pltpu.get_barrier_semaphore()
    total = jnp.int32(0)
    for valid, target in steps:
        total = total + valid.astype(jnp.int32)

        @pl.when(valid)
        def _():
            pl.semaphore_signal(barrier, inc=1, device_id=target, device_id_type=MESH)
    pl.semaphore_wait(barrier, total)
    for copy in own:
        copy.wait()

    def send(go, way, block, send_sem, recv_sem, start):
        valid, target = steps[way]

        @pl.when(jnp.logical_and(go, valid))
        def _():
            copy = pltpu.make_async_remote_copy(
                src_ref=block, dst_ref=block, send_sem=send_sem.at[way], recv_sem=recv_sem,
                device_id=target, device_id_type=MESH)
            if start:
                copy.start()
            else:
                copy.wait_send()

    def arrive(block, send_sem, recv_sem):
        pltpu.make_async_remote_copy(
            src_ref=block, dst_ref=block, send_sem=send_sem, recv_sem=recv_sem,
            device_id=steps[6][1], device_id_type=MESH).wait_recv()

    def g_event(zz, yy, xx, start):
        index = (zz * ny + yy) * nx + xx
        block = g_block(zz, yy, xx, core)
        sems = g_send.at[index]
        if start:
            @pl.when(jnp.logical_or(xx != x, jnp.logical_or(yy != y, zz != z)))
            def _():
                arrive(block, sems.at[0], g_recv.at[index])
        in_x = xx == x
        in_xy = jnp.logical_and(in_x, yy == y)
        go = functools.partial(send, block=block, send_sem=sems, recv_sem=g_recv.at[index], start=start)
        go(xx >= x, 0)
        go(xx <= x, 1)
        go(jnp.logical_and(in_x, yy >= y), 2)
        go(jnp.logical_and(in_x, yy <= y), 3)
        go(jnp.logical_and(in_xy, zz >= z), 4)
        go(jnp.logical_and(in_xy, zz <= z), 5)
        send(core >= 0, 6, block, sems, g_peer.at[index], start)

    def u_event(zz, yy, start):
        index = zz * ny + yy
        block = u_block(zz, yy)
        sems = u_send.at[index]
        if start:
            @pl.when(jnp.logical_or(yy != y, zz != z))
            def _():
                arrive(block, sems.at[0], u_recv.at[index])
        in_y = yy == y
        go = functools.partial(send, block=block, send_sem=sems, recv_sem=u_recv.at[index], start=start)
        go(yy >= y, 2)
        go(yy <= y, 3)
        go(jnp.logical_and(in_y, zz >= z), 4)
        go(jnp.logical_and(in_y, zz <= z), 5)

    def b_event(zz, yy, start):
        index = zz * ny + yy
        block = b_block(zz, yy)
        sems = b_send.at[index]
        if start:
            @pl.when(jnp.logical_or(yy != y, zz != z))
            def _():
                arrive(block, sems.at[0], b_recv.at[index])
        in_z = zz == z
        go = functools.partial(send, block=block, send_sem=sems, recv_sem=b_recv.at[index], start=start)
        go(jnp.logical_and(in_z, yy >= y), 2)
        go(jnp.logical_and(in_z, yy <= y), 3)
        go(zz >= z, 4)
        go(zz <= z, 5)

    def over_y(body):
        def run(k, carry):
            body(nearest(y, k, ny))
            return carry
        lax.fori_loop(0, ny, run, 0)

    def over_x(first, body):
        def run(k, carry):
            body(nearest(x, k, nx))
            return carry
        lax.fori_loop(first, nx, run, 0)

    top, wide = u_all.shape
    chunk = 256
    pieces = spread.shape[0] // chunk
    tile = 512
    dot = functools.partial(jnp.dot, preferred_element_type=F32)
    dot_t = functools.partial(lax.dot_general, dimension_numbers=(((0,), (0,)), ((), ())),
                              preferred_element_type=F32)

    def place(first, last):
        @pl.loop(first, last)
        def _(i):
            at = pl.multiple_of(i * chunk, chunk)
            row = lax.broadcasted_iota(jnp.int32, (chunk, across_ref.shape[1]), 0) + at
            one_hot = jnp.where(row == across_ref[...], 1.0, 0.0).astype(BF16)
            spread[pl.ds(at, chunk), :] = dot(one_hot, leaf_all[...]).astype(BF16)

    def add_diag(part, product, span):
        diag_ref[:, span] += jnp.sum(part.astype(F32) * product, axis=0, keepdims=True)

    def compute(zz, yy):
        at = pl.ds(pl.multiple_of((zz * ny + yy) * rows, rows), rows)
        cross = (-dot(g_all[at, :], u_all[...])).astype(BF16)

        @pl.when(jnp.logical_and(zz == z, yy == y))
        def _():
            cross_out[...] = cross
        projected[...] += dot_t(u_all[at, :], cross)

        @pl.loop(0, y_ref.shape[1] // tile)
        def _(j):
            span = pl.ds(pl.multiple_of(j * tile, tile), tile)
            own_part = spread[at, span]
            product = dot(g_all[at, :], spread[:top, span]) + dot(cross, spread[top:, span])
            y_ref[at, span] = (-product).astype(BF16)
            add_diag(own_part, product, span)
            low[:, span] += dot_t(cross, own_part)

    projected[...] = jnp.zeros_like(projected)
    low[...] = jnp.zeros_like(low)
    diag_ref[...] = bdiag_ref[...]

    def x_group(k):
        zz = nearest(z, k, nz)
        over_y(lambda yy: over_x(1, lambda xx: g_event(zz, yy, xx, True)))

    leaf_copy.wait()

    def travel(k, carry):
        zz = nearest(z, k, nz)
        over_y(lambda yy: g_event(zz, yy, x, True))
        over_y(lambda yy: u_event(zz, yy, True))
        over_y(lambda yy: b_event(zz, yy, True))
        place(pieces * k // nz, pieces * (k + 1) // nz)

        @pl.when(k > 1)
        def _():
            x_group(k - 2)
        return carry

    lax.fori_loop(0, nz, travel, 0)

    def group(k, carry):
        zz = nearest(z, k, nz)

        def rows_of(yy):
            def peer(xx, carry):
                index = (zz * ny + yy) * nx + xx
                arrive(g_block(zz, yy, xx, 1 - core), g_send.at[index].at[6], g_peer.at[index])
                return carry
            lax.fori_loop(0, nx, peer, 0)
            compute(zz, yy)
        over_y(rows_of)

        @pl.when(k < 2)
        def _():
            x_group(k + nz - 2)
        return carry

    lax.fori_loop(0, nz, group, 0)

    block[...] = (b_all[...].astype(F32) - projected[...]).astype(BF16)
    own_rows = pl.ds(pl.multiple_of((z * ny + y) * mid, mid), mid)
    exact = (exact_ref[...] - projected[own_rows, :]).astype(BF16)
    block[own_rows, :] = exact
    mid_out[...] = exact

    @pl.loop(0, y_ref.shape[1] // tile)
    def _(j):
        span = pl.ds(pl.multiple_of(j * tile, tile), tile)
        part = spread[top:, span]
        product = low[:, span] + dot(block[...], part)
        y_ref[top:, span] = (-product).astype(BF16)
        add_diag(part, product, span)

    def finish(zz, carry):
        def inner(yy, carry):
            u_event(zz, yy, False)
            b_event(zz, yy, False)

            def last(xx, carry):
                g_event(zz, yy, xx, False)
                return carry
            return lax.fori_loop(0, nx, last, carry)
        return lax.fori_loop(0, ny, inner, carry)

    lax.fori_loop(0, nz, finish, 0)


def gather_all(n_sep, n_sub, g_top, u_mid, b_mid, across, bdiag, u_leaf):
    nx = n_sep // 2
    ny = math.isqrt(n_sub // 2)
    nz = n_sub // ny
    top = g_top.shape[0] * n_sub
    wide = u_mid.shape[1]
    slots, columns = u_leaf.shape
    dma = pltpu.SemaphoreType.DMA
    n = nx * n_sub
    any_space = pl.BlockSpec(memory_space=pl.ANY)
    vmem = pl.BlockSpec(memory_space=pltpu.VMEM)
    return pl.pallas_call(
        functools.partial(gather_kernel, nx, ny, nz),
        out_shape=(
            jax.ShapeDtypeStruct(u_mid.shape, BF16),
            jax.ShapeDtypeStruct(b_mid.shape, BF16),
            jax.ShapeDtypeStruct((top + wide, columns), BF16),
            jax.ShapeDtypeStruct((1, columns), F32),
        ),
        in_specs=[any_space] * 3 + [vmem] * 2 + [any_space, vmem],
        out_specs=(vmem,) * 4,
        scratch_shapes=[
            pltpu.VMEM((top, top), BF16), pltpu.VMEM((top, wide), BF16), pltpu.VMEM((wide, wide), BF16),
            pltpu.VMEM((slots, columns), BF16), pltpu.VMEM((top + wide, columns), BF16),
            pltpu.VMEM((wide, columns), F32), pltpu.VMEM((wide, wide), F32), pltpu.VMEM((wide, wide), BF16),
            dma((4,)), dma((n,)), dma((n,)), dma((n, 7)),
            dma((n_sub,)), dma((n_sub, 7)), dma((n_sub,)), dma((n_sub, 7)),
        ],
        compiler_params=pltpu.CompilerParams(collective_id=0, has_side_effects=True,
                                             vmem_limit_bytes=60 * 2**20),
    )(g_top, u_mid, b_mid.astype(BF16), across, bdiag, u_leaf, b_mid)


def pick_kernel(down_ref, y_ref, off_ref):
    column = lax.broadcasted_iota(jnp.int32, (off_ref.shape[0], y_ref.shape[0]), 1)
    pick = jnp.where(column == down_ref[...], 1.0, 0.0).astype(BF16)
    off_ref[...] = jnp.dot(pick, y_ref[...], preferred_element_type=F32).astype(BF16)


def pick_rows(down, y):
    slots, (total, columns) = down.shape[0], y.shape
    tile = 256
    return pl.pallas_call(
        pick_kernel,
        grid=(slots // tile,),
        out_shape=jax.ShapeDtypeStruct((slots, columns), BF16),
        in_specs=[
            pl.BlockSpec((tile, 1), lambda i: (i, 0)),
            pl.BlockSpec((total, columns), lambda i: (0, 0), pipeline_mode=pl.Buffered(1)),
        ],
        out_specs=pl.BlockSpec((tile, columns), lambda i: (i, 0)),
        compiler_params=pltpu.CompilerParams(vmem_limit_bytes=40 * 2**20),
    )(down, y)


def shards(n_sep, n_sub, g_top, u_mid, b_mid, u_leaf, leaf_index, leaf_count, leaf_bdiag):
    slots = leaf_index.shape[1]
    live = jnp.arange(slots, dtype=jnp.int32)[None, :] < leaf_count[0]
    across = jnp.where(live, leaf_index, -1)
    cross_rows, mid_rows, y, diag = gather_all(
        n_sep, n_sub, g_top, u_mid[0], b_mid[0], across, leaf_bdiag, u_leaf[0])
    off = pick_rows(across.reshape(slots, 1), y)
    return cross_rows[None], mid_rows[None], off[None], diag


def solution(mesh):
    return jax.shard_map(
        functools.partial(shards, mesh.shape["sep"], mesh.shape["sub"]),
        mesh=mesh,
        in_specs=(
            P("sub", "sep"),
            P("sep", "sub", None),
            P("sep", "sub", None),
            P(("sep", "sub"), None, None),
            P(("sep", "sub"), None),
            P(("sep", "sub")),
            P(("sep", "sub"), None),
        ),
        out_specs=(
            P("sep", "sub", None),
            P("sep", "sub", None),
            P(("sep", "sub"), None, None),
            P(("sep", "sub"), None),
        ),
        check_vma=False,
    )
```
